1024 devices in a mesh: seq: 64 (over z, y), head: 16 (over x, core).
Axes of the slice: x: 8, y: 8, z: 8, core: 2. Of those that a mesh axis runs over, the one named last changes fastest.
Arguments:
- queries: bfloat16 [32768, 4096], P(('seq', 'head')), may hold values from -100 to 100
- keys_in: bfloat16 [32768, 4096], P(('seq', 'head')), may hold values from -16 to 16
- values_in: bfloat16 [32768, 4096], P(('seq', 'head')), may hold values from -16 to 16
- grad_out: bfloat16 [32768, 4096], P(('seq', 'head')), may hold values from -6 to 6
Outputs:
- attended: bfloat16 [32768, 4096], P(('seq', 'head'))
- grad_queries: bfloat16 [32768, 4096], P(('seq', 'head'))
- grad_keys: bfloat16 [32768, 4096], P(('seq', 'head'))
- grad_values: bfloat16 [32768, 4096], P(('seq', 'head'))
The draws below stay inside these ranges and needn't reach their ends.
All inputs are finite; a program needn't handle non-finite values.
Results may differ from the reference program's by a relative error of at most 0.0052.
Values may be sent and summed in bfloat16 or wider, within the bound.
A program may use at most 32 MiB of HBM per device.

```python
import jax
import jax.numpy as jnp
from jax import lax

HEADS = 32
HD = 128
SHARD = 512
CROWS = 16
TOKENS = 32768
N_SEQ = 64


def drifting(key, salt):
    rough = jax.random.normal(jax.random.fold_in(key, salt), (TOKENS, HEADS * HD), jnp.float32)
    slow = jax.random.normal(jax.random.fold_in(key, salt + 1), (TOKENS // 64, 1, HEADS * HD), jnp.float32)
    slow = jnp.broadcast_to(slow, (TOKENS // 64, 64, HEADS * HD)).reshape(TOKENS, HEADS * HD)
    return jnp.clip(rough + slow, -15.0, 15.0)


def draw_keys_in(key, part):
    return drifting(key, 11).astype(jnp.bfloat16)


def draw_values_in(key, part):
    return drifting(key, 31).astype(jnp.bfloat16)


def draw_queries(key, part):
    drawn = jax.random.normal(jax.random.fold_in(key, 51), (TOKENS, HEADS * HD), jnp.float32)
    drawn = jnp.clip(drawn, -6.0, 6.0)
    return drawn.astype(jnp.bfloat16)


def levels(stream_key, extent, shards, least, high):
    gain = 1.0
    for dim, parts in shards:
        draws = jax.random.uniform(jax.random.fold_in(jax.random.fold_in(stream_key, 6), dim), (parts,), jnp.float32, least / len(shards), high / len(shards))
        gain = gain * jnp.repeat(jnp.exp(draws), extent[dim] // parts).reshape((-1,) + (1,) * (len(extent) - 1 - dim))
    return gain


def scatter_about(rng, shape, spread, reach, shards=(), kind=jnp.bfloat16):
    entries = jax.random.normal(rng, shape, jnp.float32) * spread
    if len(shards) > 0:
        entries = levels(rng, shape, shards, -0.22, 0.18) * entries
    return jnp.clip(entries, min=-reach, max=reach).astype(kind)


def setup_inputs(seed: int = 0) -> dict:
    keys = jax.random.split(jax.random.key(seed), 5)
    queries = draw_queries(jax.random.fold_in(keys[4], 71), 0)
    keys_in = draw_keys_in(jax.random.fold_in(keys[4], 71), 0)
    values_in = draw_values_in(jax.random.fold_in(keys[4], 71), 0)
    grad_out = scatter_about(keys[3], (TOKENS, HEADS * HD), 1.0, 6.0, ((0, 1024),))
    return dict(queries=queries, keys_in=keys_in, values_in=values_in, grad_out=grad_out)


def reference(queries, keys_in, values_in, grad_out):
    depth = N_SEQ.bit_length() - 1
    scale_q = HD ** -0.5
    pool_size = SHARD // CROWS
    q_all = queries.reshape(N_SEQ, SHARD, HEADS, HD)
    k_all = keys_in.reshape(N_SEQ, SHARD, HEADS, HD)
    v_all = values_in.reshape(N_SEQ, SHARD, HEADS, HD)
    g_all = grad_out.reshape(N_SEQ, SHARD, HEADS, HD)
    pooled_k = jnp.mean(k_all.astype(jnp.float32).reshape(N_SEQ, CROWS, pool_size, HEADS, HD), axis=2).transpose(0, 2, 1, 3)
    pooled_v = jnp.mean(v_all.astype(jnp.float32).reshape(N_SEQ, CROWS, pool_size, HEADS, HD), axis=2).transpose(0, 2, 1, 3)
    group_k = []
    group_v = []
    for level in range(depth):
        width_here = 2 ** level
        group_k.append(jnp.mean(pooled_k.reshape(N_SEQ // width_here, width_here, HEADS, CROWS, HD), axis=1))
        group_v.append(jnp.mean(pooled_v.reshape(N_SEQ // width_here, width_here, HEADS, CROWS, HD), axis=1))
    log_counts = jnp.repeat(jnp.log(float(pool_size) * 2.0 ** jnp.arange(depth, dtype=jnp.float32)), CROWS)
    offsets = jnp.concatenate([jnp.zeros((SHARD,), jnp.float32), log_counts.astype(jnp.float32)])

    def per_device(device):
        sib_k = jnp.stack([group_k[level][(device >> level) ^ 1] for level in range(depth)], axis=1)
        sib_v = jnp.stack([group_v[level][(device >> level) ^ 1] for level in range(depth)], axis=1)
        sib_k = lax.optimization_barrier(sib_k.reshape(HEADS, depth * CROWS, HD).astype(jnp.bfloat16)).astype(jnp.float32)
        sib_v = lax.optimization_barrier(sib_v.reshape(HEADS, depth * CROWS, HD).astype(jnp.bfloat16)).astype(jnp.float32)
        query_here = q_all[device].astype(jnp.float32)
        grad_here = g_all[device].astype(jnp.float32)
        keys_full = jnp.concatenate([k_all[device].astype(jnp.float32).transpose(1, 0, 2), sib_k], axis=1)
        values_full = jnp.concatenate([v_all[device].astype(jnp.float32).transpose(1, 0, 2), sib_v], axis=1)
        scores = jnp.einsum("shd,htd->hst", query_here, keys_full) * scale_q + offsets
        probs = jax.nn.softmax(scores, axis=-1)
        probs_low = lax.optimization_barrier(probs.astype(jnp.bfloat16)).astype(jnp.float32)
        attended = jnp.einsum("hst,htd->shd", probs_low, values_full).astype(jnp.bfloat16)
        dprob = jnp.einsum("shd,htd->hst", grad_here, values_full)
        dscore = scale_q * probs * (dprob - jnp.sum(probs * dprob, axis=-1, keepdims=True))
        dscore_low = lax.optimization_barrier(dscore.astype(jnp.bfloat16)).astype(jnp.float32)
        grad_query = jnp.einsum("hst,htd->shd", dscore_low, keys_full).astype(jnp.bfloat16)
        dkeys = jnp.einsum("hst,shd->htd", dscore_low, query_here)
        dvalues = jnp.einsum("hst,shd->htd", probs_low, grad_here)
        return (attended, grad_query, dkeys[:, :SHARD], dvalues[:, :SHARD],
                dkeys[:, SHARD:].reshape(HEADS, depth, CROWS, HD), dvalues[:, SHARD:].reshape(HEADS, depth, CROWS, HD))

    results = lax.map(per_device, jnp.arange(N_SEQ, dtype=jnp.int32))
    grad_pool_k = jnp.zeros((N_SEQ, HEADS, CROWS, HD), jnp.float32)
    grad_pool_v = jnp.zeros((N_SEQ, HEADS, CROWS, HD), jnp.float32)
    device_ids = jnp.arange(N_SEQ, dtype=jnp.int32)
    for level in range(depth):
        width_here = 2 ** level
        sums_k = jnp.sum(results[4][:, :, level].reshape(N_SEQ // width_here, width_here, HEADS, CROWS, HD), axis=1)
        sums_v = jnp.sum(results[5][:, :, level].reshape(N_SEQ // width_here, width_here, HEADS, CROWS, HD), axis=1)
        grad_pool_k = grad_pool_k + sums_k[(device_ids >> level) ^ 1] / float(width_here)
        grad_pool_v = grad_pool_v + sums_v[(device_ids >> level) ^ 1] / float(width_here)
    grad_k = results[2] + jnp.repeat(grad_pool_k / float(pool_size), pool_size, axis=2)
    grad_v = results[3] + jnp.repeat(grad_pool_v / float(pool_size), pool_size, axis=2)
    attended = results[0].reshape(TOKENS, HEADS * HD)
    grad_q = results[1].reshape(TOKENS, HEADS * HD)
    grad_k = grad_k.transpose(0, 2, 1, 3).reshape(TOKENS, HEADS * HD).astype(jnp.bfloat16)
    grad_v = grad_v.transpose(0, 2, 1, 3).reshape(TOKENS, HEADS * HD).astype(jnp.bfloat16)
    return (attended, grad_q, grad_k, grad_v)
```

```python
import functools
import math

import jax
import jax.numpy as jnp
from jax import lax
from jax.experimental import pallas as pl
from jax.experimental.pallas import tpu as pltpu
from jax.sharding import PartitionSpec as P

HD = 128
MESH = pl.DeviceIdType.MESH
F32 = jnp.float32
BF16 = jnp.bfloat16

S_POOL, S_K, S_V, S_Q, S_G, S_YF, S_ZF, S_ZB, S_YB, S_OUT = 0, 1, 2, 3, 5, 7, 9, 11, 13, 15
N_SEMS = 19


def flip(index, mask):
    out = index
    bit = 1
    while bit <= mask:
        if mask & bit:
            out = out + bit * (1 - 2 * ((index // bit) % 2))
        bit *= 2
    return out


def kernel(sizes, *refs):
    nx, ny, nz = sizes
    (q_in, k_in, v_in, g_in, o_out, dq_out, dk_out, dv_out,
     kl, vl, ps, pr, qr, kr, vr, gr, yr, zr, kc, vc, zs, zb, ys, yb,
     os, dqs, dks, dvs, dka, dva, dkc, dvc, local_sem, send, recv) = refs
    ins = (q_in, k_in, v_in, g_in)
    outs = (o_out, dq_out, dk_out, dv_out)
    nh = nx * 2
    rows = q_in.shape[0]
    shard = nh * rows
    ly, lz = ny.bit_length() - 1, nz.bit_length() - 1
    levels = ly + lz
    crows = nh
    scale = HD ** (-0.5)

    s_me = lax.axis_index("seq")
    h_me = lax.axis_index("head")
    y_me, z_me = s_me % ny, s_me // ny
    x_me, c_me = h_me // 2, h_me % 2

    def ahead(slot):
        k, f = slot // 2, slot % 2
        return ((x_me + k) % nx) * 2 + (c_me if f == 0 else 1 - c_me)

    def behind(slot):
        k, f = slot // 2, slot % 2
        return ((x_me + nx - k) % nx) * 2 + (c_me if f == 0 else 1 - c_me)

    order = []
    for k in range(nx // 2, -1, -1):
        for kk in dict.fromkeys((k, (nx - k) % nx)):
            order += [2 * kk, 2 * kk + 1]
    order = [s for s in order if s != 0]

    def y_dev(k):
        return (z_me * ny + flip(y_me, k), h_me)

    def z_dev(k):
        return (flip(z_me, k) * ny + y_me, h_me)

    kcopy = pltpu.make_async_copy(k_in, kl, local_sem.at[0])
    vcopy = pltpu.make_async_copy(v_in, vl, local_sem.at[1])
    kcopy.start()
    vcopy.start()
    barrier = pltpu.get_barrier_semaphore()
    for s in order:
        pl.semaphore_signal(barrier, inc=1, device_id=(s_me, ahead(s)), device_id_type=MESH)
    for k in range(1, ny):
        pl.semaphore_signal(barrier, inc=1, device_id=y_dev(k), device_id_type=MESH)
    for k in range(1, nz):
        pl.semaphore_signal(barrier, inc=1, device_id=z_dev(k), device_id_type=MESH)

    kcopy.wait()
    vcopy.wait()
    for d in range(nh):
        for h in range(2):
            cols = pl.ds((d * 2 + h) * HD, HD)
            for kv, ref in enumerate((kl, vl)):
                mean = jnp.sum(ref[:, cols].astype(F32), axis=0, keepdims=True) * (1.0 / rows)
                ps[d, pl.ds(h * 2 + kv, 1), :] = mean

    pl.semaphore_wait(barrier, len(order) + ny - 1 + nz - 1)

    def remote(src, dst, sem, device):
        pltpu.make_async_remote_copy(
            src_ref=src, dst_ref=dst, send_sem=send.at[sem], recv_sem=recv.at[sem],
            device_id=device, device_id_type=MESH,
        ).start()

    def drain(ref, sem):
        pltpu.make_async_copy(ref, ref, sem).wait()

    for s in order:
        d = ahead(s)
        remote(ps.at[d], pr.at[s], S_POOL, (s_me, d))
    pr[0] = ps[h_me]

    def scatter_in(src, dst, sem, first, width):
        def piece(d):
            start = pl.multiple_of(d * 2 * HD + first, HD)
            return src.at[:, pl.ds(start, width)]

        for s in order:
            d = ahead(s)
            remote(piece(d), dst.at[pl.ds(s * rows, rows), pl.ds(first, width)], sem, (s_me, d))
        pltpu.make_async_copy(
            piece(h_me), dst.at[pl.ds(0, rows), pl.ds(first, width)], recv.at[sem]
        ).start()

    scatter_in(k_in, kr, S_K, 0, 2 * HD)
    scatter_in(v_in, vr, S_V, 0, 2 * HD)
    for h in range(2):
        scatter_in(q_in, qr, S_Q + h, h * HD, HD)
        scatter_in(g_in, gr, S_G + h, h * HD, HD)

    drain(pr.at[pl.ds(1, nh - 1)], recv.at[S_POOL])
    for h in range(2):
        for kv in range(2):
            yr[h, 0, pl.ds(kv * crows, crows), :] = pr[:, h * 2 + kv, :]
        for k in range(1, ny):
            remote(yr.at[h, 0], yr.at[h, k], S_YF + h, y_dev(k))

    def siblings(h, got, count, base):
        for j in range(count):
            width = 1 << j
            total = got[h, width]
            for k in range(width + 1, 2 * width):
                total = total + got[h, k]
            mean = (total * (1.0 / width)).astype(BF16)
            kc[h, pl.ds((base + j) * crows, crows), :] = mean[:crows]
            vc[h, pl.ds((base + j) * crows, crows), :] = mean[crows:]

    for h in range(2):
        drain(yr.at[h, pl.ds(1, ny - 1)], recv.at[S_YF + h])
        total = yr[h, 0]
        for k in range(1, ny):
            total = total + yr[h, k]
        zr[h, 0] = total * (1.0 / ny)
        for k in range(1, nz):
            remote(zr.at[h, 0], zr.at[h, k], S_ZF + h, z_dev(k))
        siblings(h, yr, ly, 0)
    for h in range(2):
        drain(zr.at[h, pl.ds(1, nz - 1)], recv.at[S_ZF + h])
        siblings(h, zr, lz, ly)

    drain(kr, recv.at[S_K])
    drain(vr, recv.at[S_V])

    row_level = lax.broadcasted_iota(jnp.int32, (levels * crows, 1), 0) // crows
    offsets = jnp.zeros((levels * crows, 1), F32)
    for j in range(levels):
        offsets = jnp.where(row_level == j, math.log(float(rows) * 2.0**j), offsets)

    nt = (((1,), (1,)), ((), ()))
    nn = (((1,), (0,)), ((), ()))
    tn = (((0,), (0,)), ((), ()))

    def dot(a, b, dims):
        return lax.dot_general(a, b, dims, preferred_element_type=F32)

    def compute(h):
        hc = pl.ds(h * HD, HD)
        block = min(shard, 256)
        kf, vf = kr[:, hc], vr[:, hc]
        kcv, vcv = kc[h], vc[h]
        for b in range(shard // block):
            br = pl.ds(b * block, block)
            q, g = qr[br, hc], gr[br, hc]
            sf = dot(kf, q, nt) * scale
            sc = dot(kcv, q, nt) * scale + offsets
            top = jnp.maximum(
                jnp.max(sf, axis=0, keepdims=True), jnp.max(sc, axis=0, keepdims=True)
            )
            pf, pc = jnp.exp(sf - top), jnp.exp(sc - top)
            norm = 1.0 / (
                jnp.sum(pf, axis=0, keepdims=True) + jnp.sum(pc, axis=0, keepdims=True)
            )
            pf, pc = pf * norm, pc * norm
            pfl, pcl = pf.astype(BF16), pc.astype(BF16)
            os[h, br, :] = (dot(pfl, vf, tn) + dot(pcl, vcv, tn)).astype(BF16)
            df, dc = dot(vf, g, nt), dot(vcv, g, nt)
            delta = jnp.sum(pf * df, axis=0, keepdims=True) + jnp.sum(
                pc * dc, axis=0, keepdims=True
            )
            dsf = (scale * pf * (df - delta)).astype(BF16)
            dsc = (scale * pc * (dc - delta)).astype(BF16)
            dqs[h, br, :] = (dot(dsf, kf, tn) + dot(dsc, kcv, tn)).astype(BF16)
            for acc, val in (
                (dka, dot(dsf, q, nn)),
                (dva, dot(pfl, g, nn)),
                (dkc, dot(dsc, q, nn)),
                (dvc, dot(pcl, g, nn)),
            ):
                if b == 0:
                    acc[h] = val
                else:
                    acc[h] += val

    def scatter_out(src, h, which):
        out = outs[which]
        start = pl.multiple_of((h_me * 2 + h) * HD, HD)
        there = out.at[:, pl.ds(start, HD)]
        for s in order:
            remote(src.at[h, pl.ds(s * rows, rows), :], there, S_OUT + which, (s_me, behind(s)))
        pltpu.make_async_copy(src.at[h, pl.ds(0, rows), :], there, recv.at[S_OUT + which]).start()

    for h in range(2):
        drain(qr.at[:, pl.ds(h * HD, HD)], recv.at[S_Q + h])
        drain(gr.at[:, pl.ds(h * HD, HD)], recv.at[S_G + h])
        compute(h)
        for j in range(lz):
            at = pl.ds((ly + j) * crows, crows)
            weight = 2.0 ** -(ly + j)
            zs[h, j, pl.ds(0, crows), :] = dkc[h, at, :] * weight
            zs[h, j, pl.ds(crows, crows), :] = dvc[h, at, :] * weight
        for k in range(1, nz):
            remote(zs.at[h, k.bit_length() - 1], zb.at[h, k], S_ZB + h, z_dev(k))
        scatter_out(os, h, 0)
        scatter_out(dqs, h, 1)

    for h in range(2):
        drain(zb.at[h, pl.ds(1, nz - 1)], recv.at[S_ZB + h])
        total = zb[h, 1]
        for k in range(2, nz):
            total = total + zb[h, k]
        yb[h, 0] = total
        for j in range(ly):
            at = pl.ds(j * crows, crows)
            weight = 2.0**-j
            ys[h, j, pl.ds(0, crows), :] = total[:crows] + dkc[h, at, :] * weight
            ys[h, j, pl.ds(crows, crows), :] = total[crows:] + dvc[h, at, :] * weight
        for k in range(1, ny):
            remote(ys.at[h, k.bit_length() - 1], yb.at[h, k], S_YB + h, y_dev(k))
    for h in range(2):
        drain(yb.at[h, pl.ds(1, ny - 1)], recv.at[S_YB + h])
        total = yb[h, 0]
        for k in range(1, ny):
            total = total + yb[h, k]
        total = total * (1.0 / rows)
        for which, (acc, dst, base) in enumerate(((dka, dks, 0), (dva, dvs, crows))):
            for s in range(nh):
                at = pl.ds(s * rows, rows)
                dst[h, at, :] = (acc[h, at, :] + total[base + s : base + s + 1]).astype(BF16)
            scatter_out(dst, h, 2 + which)

    for which, out in enumerate(outs):
        drain(out, recv.at[S_OUT + which])

    drain(pr.at[pl.ds(1, nh - 1)], send.at[S_POOL])
    part = pl.ds(0, shard - rows)
    drain(kr.at[part], send.at[S_K])
    drain(vr.at[part], send.at[S_V])
    for h in range(2):
        hc = pl.ds(h * HD, HD)
        drain(qr.at[part, hc], send.at[S_Q + h])
        drain(gr.at[part, hc], send.at[S_G + h])
        drain(yr.at[h, pl.ds(1, ny - 1)], send.at[S_YF + h])
        drain(zr.at[h, pl.ds(1, nz - 1)], send.at[S_ZF + h])
        drain(zb.at[h, pl.ds(1, nz - 1)], send.at[S_ZB + h])
        drain(yb.at[h, pl.ds(1, ny - 1)], send.at[S_YB + h])
    for which in range(4):
        drain(kr.at[part], send.at[S_OUT + which])


def solution(mesh):
    seq, head = mesh.shape["seq"], mesh.shape["head"]
    depth = seq.bit_length() - 1
    ny = 1 << (depth // 2)
    nz = seq // ny
    nx = head // 2

    def on_device(queries, keys_in, values_in, grad_out):
        rows, width = queries.shape
        shard = rows * head
        levels = depth
        here = jax.ShapeDtypeStruct((rows, width), BF16)
        anywhere = pl.BlockSpec(memory_space=pl.ANY)
        vm = pltpu.VMEM
        return pl.pallas_call(
            functools.partial(kernel, (nx, ny, nz)),
            out_shape=(here,) * 4,
            in_specs=[anywhere] * 4,
            out_specs=(anywhere,) * 4,
            scratch_shapes=[
                vm((rows, width), BF16),
                vm((rows, width), BF16),
                vm((head, 8, HD), F32),
                vm((head, 8, HD), F32),
                vm((shard, 2 * HD), BF16),
                vm((shard, 2 * HD), BF16),
                vm((shard, 2 * HD), BF16),
                vm((shard, 2 * HD), BF16),
                vm((2, ny, 2 * head, HD), F32),
                vm((2, nz, 2 * head, HD), F32),
                vm((2, levels * head, HD), BF16),
                vm((2, levels * head, HD), BF16),
                vm((2, depth - depth // 2, 2 * head, HD), F32),
                vm((2, nz, 2 * head, HD), F32),
                vm((2, depth // 2, 2 * head, HD), F32),
                vm((2, ny, 2 * head, HD), F32),
                vm((2, shard, HD), BF16),
                vm((2, shard, HD), BF16),
                vm((2, shard, HD), BF16),
                vm((2, shard, HD), BF16),
                vm((2, shard, HD), F32),
                vm((2, shard, HD), F32),
                vm((2, levels * head, HD), F32),
                vm((2, levels * head, HD), F32),
                pltpu.SemaphoreType.DMA((2,)),
                pltpu.SemaphoreType.DMA((N_SEMS,)),
                pltpu.SemaphoreType.DMA((N_SEMS,)),
            ],
            compiler_params=pltpu.CompilerParams(
                collective_id=0, has_side_effects=True, vmem_limit_bytes=40 * 1024 * 1024
            ),
        )(queries, keys_in, values_in, grad_out)

    placed = P(("seq", "head"), None)
    return jax.shard_map(
        on_device, mesh=mesh, in_specs=(placed,) * 4, out_specs=(placed,) * 4, check_vma=False
    )
```

```python
import functools
import math

import jax
import jax.numpy as jnp
from jax import lax
from jax.experimental import pallas as pl
from jax.experimental.pallas import tpu as pltpu
from jax.sharding import PartitionSpec as P

HD = 128
MESH = pl.DeviceIdType.MESH
F32 = jnp.float32
BF16 = jnp.bfloat16

S_POOL, S_K, S_V, S_Q, S_G, S_YF, S_ZF, S_ZB, S_YB, S_OUT, S_GX = 0, 1, 2, 3, 5, 7, 9, 11, 13, 15, 19
N_SEMS = 20


def flip(index, mask):
    out = index
    bit = 1
    while bit <= mask:
        if mask & bit:
            out = out + bit * (1 - 2 * ((index // bit) % 2))
        bit *= 2
    return out


def kernel(sizes, *refs):
    nx, ny, nz = sizes
    (q_in, k_in, v_in, g_in, o_out, dq_out, dk_out, dv_out, gx_out,
     kl, vl, ps, pr, qr, kr, vr, gr, yr, zr, kc, vc, zs, zb, ys, yb,
     gs, os, dqs, dks, dvs, dka, dva, dkc, dvc, local_sem, send, recv, go) = refs
    ins = (q_in, k_in, v_in, g_in)
    outs = (o_out, dq_out, dk_out, dv_out)
    nh = nx * 2
    rows = q_in.shape[0]
    shard = nh * rows
    ly, lz = ny.bit_length() - 1, nz.bit_length() - 1
    levels = ly + lz
    crows = nh
    scale = HD ** (-0.5)

    s_me = lax.axis_index("seq")
    h_me = lax.axis_index("head")
    y_me, z_me = s_me % ny, s_me // ny
    x_me, c_me = h_me // 2, h_me % 2

    def ahead(slot):
        k, f = slot // 2, slot % 2
        return ((x_me + k) % nx) * 2 + (c_me if f == 0 else 1 - c_me)

    def behind(slot):
        k, f = slot // 2, slot % 2
        return ((x_me + nx - k) % nx) * 2 + (c_me if f == 0 else 1 - c_me)

    order = []
    for k in range(nx // 2, -1, -1):
        for kk in dict.fromkeys((k, (nx - k) % nx)):
            order += [2 * kk, 2 * kk + 1]
    order = [s for s in order if s != 0]

    def y_dev(k):
        return (z_me * ny + flip(y_me, k), h_me)

    def z_dev(k):
        return (flip(z_me, k) * ny + y_me, h_me)

    kcopy = pltpu.make_async_copy(k_in, kl, local_sem.at[0])
    vcopy = pltpu.make_async_copy(v_in, vl, local_sem.at[1])
    kcopy.start()
    vcopy.start()

    barrier = pltpu.get_barrier_semaphore()
    for s in order:
        pl.semaphore_signal(barrier, inc=1, device_id=(s_me, ahead(s)), device_id_type=MESH)

    kcopy.wait()
    vcopy.wait()
    for d in range(nh):
        for h in range(2):
            cols = pl.ds((d * 2 + h) * HD, HD)
            for kv, ref in enumerate((kl, vl)):
                mean = jnp.sum(ref[:, cols].astype(F32), axis=0, keepdims=True) * (1.0 / rows)
                ps[d, pl.ds(h * 2 + kv, 1), :] = mean

    lines = [y_dev(k)[0] for k in range(1, ny)] + [z_dev(k)[0] for k in range(1, nz)]
    pl.semaphore_wait(barrier, len(order) + jnp.where(h_me == 0, len(lines), 0))

    @pl.when(h_me == 1)
    def _():
        for line in lines:
            pl.semaphore_signal(barrier, inc=1, device_id=(line, 0), device_id_type=MESH)

    @pl.when(h_me == 0)
    def _():
        for d in range(1, nh):
            pl.semaphore_signal(go, inc=1, device_id=(s_me, d), device_id_type=MESH)

    def remote(src, dst, sem, device):
        pltpu.make_async_remote_copy(
            src_ref=src, dst_ref=dst, send_sem=send.at[sem], recv_sem=recv.at[sem],
            device_id=device, device_id_type=MESH,
        ).start()

    def drain(ref, sem):
        pltpu.make_async_copy(ref, ref, sem).wait()

    def scatter_in(src, dst, sem, first, width):
        def piece(d):
            start = pl.multiple_of(d * 2 * HD + first, HD)
            return src.at[:, pl.ds(start, width)]

        for s in order:
            d = ahead(s)
            remote(piece(d), dst.at[pl.ds(s * rows, rows), pl.ds(first, width)], sem, (s_me, d))
        pltpu.make_async_copy(
            piece(h_me), dst.at[pl.ds(0, rows), pl.ds(first, width)], recv.at[sem]
        ).start()

    for s in order:
        d = ahead(s)
        remote(ps.at[d], pr.at[s], S_POOL, (s_me, d))
    pr[0] = ps[h_me]

    scatter_in(k_in, kr, S_K, 0, 2 * HD)
    scatter_in(v_in, vr, S_V, 0, 2 * HD)
    for h in range(2):
        scatter_in(q_in, qr, S_Q + h, h * HD, HD)
        scatter_in(g_in, gr, S_G + h, h * HD, HD)

    drain(pr.at[pl.ds(1, nh - 1)], recv.at[S_POOL])

    @pl.when(h_me != 0)
    def _():
        pl.semaphore_wait(go, 1)

    for h in range(2):
        for kv in range(2):
            yr[h, 0, pl.ds(kv * crows, crows), :] = pr[:, h * 2 + kv, :]
        for k in range(1, ny):
            remote(yr.at[h, 0], yr.at[h, k], S_YF + h, y_dev(k))

    def siblings(h, got, count, base):
        for j in range(count):
            width = 1 << j
            total = got[h, width]
            for k in range(width + 1, 2 * width):
                total = total + got[h, k]
            mean = (total * (1.0 / width)).astype(BF16)
            kc[h, pl.ds((base + j) * crows, crows), :] = mean[:crows]
            vc[h, pl.ds((base + j) * crows, crows), :] = mean[crows:]

    for h in range(2):
        drain(yr.at[h, pl.ds(1, ny - 1)], recv.at[S_YF + h])
        total = yr[h, 0]
        for k in range(1, ny):
            total = total + yr[h, k]
        zr[h, 0] = total * (1.0 / ny)
        for k in range(1, nz):
            remote(zr.at[h, 0], zr.at[h, k], S_ZF + h, z_dev(k))
        siblings(h, yr, ly, 0)
    row_level = lax.broadcasted_iota(jnp.int32, (levels * crows, 1), 0) // crows
    offsets = jnp.zeros((levels * crows, 1), F32)
    for j in range(levels):
        offsets = jnp.where(row_level == j, math.log(float(rows) * 2.0**j), offsets)

    nt = (((1,), (1,)), ((), ()))
    nn = (((1,), (0,)), ((), ()))
    tn = (((0,), (0,)), ((), ()))

    def dot(a, b, dims):
        return lax.dot_general(a, b, dims, preferred_element_type=F32)

    def compute(h, between):
        hc = pl.ds(h * HD, HD)
        block = min(shard, 256)
        kf, vf = kr[:, hc], vr[:, hc]
        kcv, vcv = kc[h], vc[h]
        for b in range(shard // block):
            if b == shard // block - 1 and between is not None:
                between()
            br = pl.ds(b * block, block)
            q, g = qr[br, hc], gr[br, hc]
            sf = dot(kf, q, nt) * scale
            sc = dot(kcv, q, nt) * scale + offsets
            top = jnp.maximum(
                jnp.max(sf, axis=0, keepdims=True), jnp.max(sc, axis=0, keepdims=True)
            )
            pf, pc = jnp.exp(sf - top), jnp.exp(sc - top)
            norm = 1.0 / (
                jnp.sum(pf, axis=0, keepdims=True) + jnp.sum(pc, axis=0, keepdims=True)
            )
            pf, pc = pf * norm, pc * norm
            pfl, pcl = pf.astype(BF16), pc.astype(BF16)
            os[h, br, :] = (dot(pfl, vf, tn) + dot(pcl, vcv, tn)).astype(BF16)
            df, dc = dot(vf, g, nt), dot(vcv, g, nt)
            delta = jnp.sum(pf * df, axis=0, keepdims=True) + jnp.sum(
                pc * dc, axis=0, keepdims=True
            )
            dsf = (scale * pf * (df - delta)).astype(BF16)
            dsc = (scale * pc * (dc - delta)).astype(BF16)
            dqs[h, br, :] = (dot(dsf, kf, tn) + dot(dsc, kcv, tn)).astype(BF16)
            for acc, val in (
                (dka, dot(dsf, q, nn)),
                (dva, dot(pfl, g, nn)),
                (dkc, dot(dsc, q, nn)),
                (dvc, dot(pcl, g, nn)),
            ):
                if b == 0:
                    acc[h] = val
                else:
                    acc[h] += val

    def scatter_out(src, h, which):
        out = outs[which]
        start = pl.multiple_of((h_me * 2 + h) * HD, HD)
        there = out.at[:, pl.ds(start, HD)]
        for s in order:
            remote(src.at[h, pl.ds(s * rows, rows), :], there, S_OUT + which, (s_me, behind(s)))
        pltpu.make_async_copy(src.at[h, pl.ds(0, rows), :], there, recv.at[S_OUT + which]).start()

    def back_along_y(h):
        drain(zb.at[h, pl.ds(1, nz - 1)], recv.at[S_ZB + h])
        total = zb[h, 1]
        for k in range(2, nz):
            total = total + zb[h, k]
        yb[h, 0] = total
        for j in range(ly):
            at = pl.ds(j * crows, crows)
            weight = 2.0**-j
            ys[h, j, pl.ds(0, crows), :] = total[:crows] + dkc[h, at, :] * weight
            ys[h, j, pl.ds(crows, crows), :] = total[crows:] + dvc[h, at, :] * weight
        for k in range(1, ny):
            remote(ys.at[h, k.bit_length() - 1], yb.at[h, k], S_YB + h, y_dev(k))

    drain(kr, recv.at[S_K])
    drain(vr, recv.at[S_V])
    for h in range(2):
        drain(zr.at[h, pl.ds(1, nz - 1)], recv.at[S_ZF + h])
        siblings(h, zr, lz, ly)
        drain(qr.at[:, pl.ds(h * HD, HD)], recv.at[S_Q + h])
        drain(gr.at[:, pl.ds(h * HD, HD)], recv.at[S_G + h])
        compute(h, (lambda: back_along_y(0)) if h else None)
        for j in range(lz):
            at = pl.ds((ly + j) * crows, crows)
            weight = 2.0 ** -(ly + j)
            zs[h, j, pl.ds(0, crows), :] = dkc[h, at, :] * weight
            zs[h, j, pl.ds(crows, crows), :] = dvc[h, at, :] * weight
        for k in range(1, nz):
            remote(zs.at[h, k.bit_length() - 1], zb.at[h, k], S_ZB + h, z_dev(k))
        dks[h] = dka[h].astype(BF16)
        dvs[h] = dva[h].astype(BF16)
        for which, staged in enumerate((os, dqs, dks, dvs)):
            scatter_out(staged, h, which)

    back_along_y(1)
    for h in range(2):
        drain(yb.at[h, pl.ds(1, ny - 1)], recv.at[S_YB + h])
        total = yb[h, 0]
        for k in range(1, ny):
            total = total + yb[h, k]
        total = total * (1.0 / rows)
        gs[:, h * 2, :] = total[:crows]
        gs[:, h * 2 + 1, :] = total[crows:]
    for s in order:
        remote(gs.at[s], gx_out.at[h_me], S_GX, (s_me, behind(s)))
    pltpu.make_async_copy(gs.at[0], gx_out.at[h_me], recv.at[S_GX]).start()

    for which, out in enumerate(outs):
        drain(out, recv.at[S_OUT + which])
    drain(gx_out, recv.at[S_GX])

    drain(pr.at[pl.ds(1, nh - 1)], send.at[S_POOL])
    part = pl.ds(0, shard - rows)
    drain(kr.at[part], send.at[S_K])
    drain(vr.at[part], send.at[S_V])
    for h in range(2):
        hc = pl.ds(h * HD, HD)
        drain(qr.at[part, hc], send.at[S_Q + h])
        drain(gr.at[part, hc], send.at[S_G + h])
        drain(yr.at[h, pl.ds(1, ny - 1)], send.at[S_YF + h])
        drain(zr.at[h, pl.ds(1, nz - 1)], send.at[S_ZF + h])
        drain(zb.at[h, pl.ds(1, nz - 1)], send.at[S_ZB + h])
        drain(yb.at[h, pl.ds(1, ny - 1)], send.at[S_YB + h])
    for which in range(4):
        drain(kr.at[part], send.at[S_OUT + which])
    drain(gs.at[pl.ds(1, nh - 1)], send.at[S_GX])


def put_out(*refs):
    arrived, placed = refs[:5], refs[5:9]
    staged, pooled, sems = refs[9:]
    ins = [staged.at[i] for i in range(4)] + [pooled]
    first = [pltpu.make_async_copy(arrived[i], ins[i], sems.at[0, i]) for i in range(5)]
    last = [pltpu.make_async_copy(staged.at[i], placed[i], sems.at[1, i]) for i in range(4)]
    for copy in first:
        copy.start()
    for i in range(2):
        first[i].wait()
        last[i].start()
    first[4].wait()
    for kv in range(2):
        first[2 + kv].wait()
        for d in range(pooled.shape[0]):
            for h in range(2):
                cols = pl.ds((d * 2 + h) * HD, HD)
                row = pooled[d, pl.ds(h * 2 + kv, 1), :]
                staged[2 + kv, :, cols] = (staged[2 + kv, :, cols].astype(F32) + row).astype(BF16)
        last[2 + kv].start()
    for copy in last:
        copy.wait()


def solution(mesh):
    seq, head = mesh.shape["seq"], mesh.shape["head"]
    depth = seq.bit_length() - 1
    ny = 1 << (depth // 2)
    nz = seq // ny
    nx = head // 2

    def on_device(queries, keys_in, values_in, grad_out):
        rows, width = queries.shape
        shard = rows * head
        levels = depth
        here = jax.ShapeDtypeStruct((rows, width), BF16)
        anywhere = pl.BlockSpec(memory_space=pl.ANY)
        vm = pltpu.VMEM
        results = pl.pallas_call(
            functools.partial(kernel, (nx, ny, nz)),
            out_shape=(here,) * 4 + (jax.ShapeDtypeStruct((head, 4, HD), F32),),
            in_specs=[anywhere] * 4,
            out_specs=(anywhere,) * 5,
            scratch_shapes=[
                vm((rows, width), BF16),
                vm((rows, width), BF16),
                vm((head, 4, HD), F32),
                vm((head, 4, HD), F32),
                vm((shard, 2 * HD), BF16),
                vm((shard, 2 * HD), BF16),
                vm((shard, 2 * HD), BF16),
                vm((shard, 2 * HD), BF16),
                vm((2, ny, 2 * head, HD), F32),
                vm((2, nz, 2 * head, HD), F32),
                vm((2, levels * head, HD), BF16),
                vm((2, levels * head, HD), BF16),
                vm((2, depth - depth // 2, 2 * head, HD), F32),
                vm((2, nz, 2 * head, HD), F32),
                vm((2, depth // 2, 2 * head, HD), F32),
                vm((2, ny, 2 * head, HD), F32),
                vm((head, 4, HD), F32),
                vm((2, shard, HD), BF16),
                vm((2, shard, HD), BF16),
                vm((2, shard, HD), BF16),
                vm((2, shard, HD), BF16),
                vm((2, shard, HD), F32),
                vm((2, shard, HD), F32),
                vm((2, levels * head, HD), F32),
                vm((2, levels * head, HD), F32),
                pltpu.SemaphoreType.DMA((2,)),
                pltpu.SemaphoreType.DMA((N_SEMS,)),
                pltpu.SemaphoreType.DMA((N_SEMS,)),
                pltpu.SemaphoreType.REGULAR,
            ],
            compiler_params=pltpu.CompilerParams(
                collective_id=0, has_side_effects=True, vmem_limit_bytes=67043328
            ),
        )(queries, keys_in, values_in, grad_out)
        return pl.pallas_call(
            put_out,
            out_shape=(here,) * 4,
            in_specs=[anywhere] * 5,
            out_specs=(anywhere,) * 4,
            scratch_shapes=[
                vm((4, rows, width), BF16),
                vm((head, 4, HD), F32),
                pltpu.SemaphoreType.DMA((2, 5)),
            ],
            compiler_params=pltpu.CompilerParams(vmem_limit_bytes=67043328),
        )(*results)

    placed = P(("seq", "head"), None)
    return jax.shard_map(
        on_device, mesh=mesh, in_specs=(placed,) * 4, out_specs=(placed,) * 4, check_vma=False
    )
```

```python
import functools
import math

import jax
import jax.numpy as jnp
from jax import lax
from jax.experimental import pallas as pl
from jax.experimental.pallas import tpu as pltpu
from jax.sharding import PartitionSpec as P

HD = 128
MESH = pl.DeviceIdType.MESH
F32 = jnp.float32
BF16 = jnp.bfloat16

S_POOL, S_K, S_V, S_Q, S_G, S_YF, S_ZF, S_ZB, S_YB, S_OUT, S_GX = 0, 1, 2, 3, 5, 7, 9, 11, 13, 15, 19
N_SEMS = 20


def flip(index, mask):
    out = index
    bit = 1
    while bit <= mask:
        if mask & bit:
            out = out + bit * (1 - 2 * ((index // bit) % 2))
        bit *= 2
    return out


def kernel(sizes, *refs):
    nx, ny, nz = sizes
    (q_in, k_in, v_in, g_in, o_out, dq_out, dk_out, dv_out, gx_out,
     kl, vl, ps, pr, qr, kr, vr, gr, yr, zr, kc, vc, zs, zb, ys, yb,
     za, pk, dsk, gs, os, dqs, dks, dvs, dkc, dvc, local_sem, send, recv, go) = refs
    ins = (q_in, k_in, v_in, g_in)
    outs = (o_out, dq_out, dk_out, dv_out)
    nh = nx * 2
    rows = q_in.shape[0]
    shard = nh * rows
    ly, lz = ny.bit_length() - 1, nz.bit_length() - 1
    levels = ly + lz
    crows = nh
    scale = HD ** (-0.5)

    s_me = lax.axis_index("seq")
    h_me = lax.axis_index("head")
    y_me, z_me = s_me % ny, s_me // ny
    x_me, c_me = h_me // 2, h_me % 2

    def ahead(slot):
        k, f = slot // 2, slot % 2
        return ((x_me + k) % nx) * 2 + (c_me if f == 0 else 1 - c_me)

    def behind(slot):
        k, f = slot // 2, slot % 2
        return ((x_me + nx - k) % nx) * 2 + (c_me if f == 0 else 1 - c_me)

    order = []
    for k in range(nx // 2, -1, -1):
        for kk in dict.fromkeys((k, (nx - k) % nx)):
            order += [2 * kk, 2 * kk + 1]
    order = [s for s in order if s != 0]

    def far_first(count):
        return sorted(range(1, count), key=lambda k: (-min(k, count - k), k))

    def y_dev(k):
        return (z_me * ny + flip(y_me, k), h_me)

    def z_dev(k):
        return (flip(z_me, k) * ny + y_me, h_me)

    kcopy = pltpu.make_async_copy(k_in, kl, local_sem.at[0])
    vcopy = pltpu.make_async_copy(v_in, vl, local_sem.at[1])
    kcopy.start()
    vcopy.start()

    barrier = pltpu.get_barrier_semaphore()
    for s in order:
        pl.semaphore_signal(barrier, inc=1, device_id=(s_me, ahead(s)), device_id_type=MESH)

    kcopy.wait()
    vcopy.wait()
    for d in range(nh):
        for h in range(2):
            cols = pl.ds((d * 2 + h) * HD, HD)
            for kv, ref in enumerate((kl, vl)):
                mean = jnp.sum(ref[:, cols].astype(F32), axis=0, keepdims=True) * (1.0 / rows)
                ps[d, pl.ds(h * 2 + kv, 1), :] = mean

    lines = [y_dev(k)[0] for k in range(1, ny)] + [z_dev(k)[0] for k in range(1, nz)]
    pl.semaphore_wait(barrier, len(order) + jnp.where(h_me == 0, len(lines), 0))

    @pl.when(h_me == 1)
    def _():
        for line in lines:
            pl.semaphore_signal(barrier, inc=1, device_id=(line, 0), device_id_type=MESH)

    @pl.when(h_me == 0)
    def _():
        for d in range(1, nh):
            pl.semaphore_signal(go, inc=1, device_id=(s_me, d), device_id_type=MESH)

    def remote(src, dst, sem, device):
        pltpu.make_async_remote_copy(
            src_ref=src, dst_ref=dst, send_sem=send.at[sem], recv_sem=recv.at[sem],
            device_id=device, device_id_type=MESH,
        ).start()

    def drain(ref, sem):
        pltpu.make_async_copy(ref, ref, sem).wait()

    def scatter_in(src, dst, sem, first, width):
        def piece(d):
            start = pl.multiple_of(d * 2 * HD + first, HD)
            return src.at[:, pl.ds(start, width)]

        for s in order:
            d = ahead(s)
            remote(piece(d), dst.at[pl.ds(s * rows, rows), pl.ds(first, width)], sem, (s_me, d))
        pltpu.make_async_copy(
            piece(h_me), dst.at[pl.ds(0, rows), pl.ds(first, width)], recv.at[sem]
        ).start()

    for s in order:
        d = ahead(s)
        remote(ps.at[d], pr.at[s], S_POOL, (s_me, d))
    pr[0] = ps[h_me]

    scatter_in(k_in, kr, S_K, 0, 2 * HD)
    scatter_in(v_in, vr, S_V, 0, 2 * HD)
    for h in range(2):
        scatter_in(q_in, qr, S_Q + h, h * HD, HD)
        scatter_in(g_in, gr, S_G + h, h * HD, HD)

    drain(pr.at[pl.ds(1, nh - 1)], recv.at[S_POOL])

    @pl.when(h_me != 0)
    def _():
        pl.semaphore_wait(go, 1)

    for h in range(2):
        for kv in range(2):
            yr[h, 0, pl.ds(kv * crows, crows), :] = pr[:, h * 2 + kv, :]
        for k in far_first(ny):
            remote(yr.at[h, 0], yr.at[h, k], S_YF + h, y_dev(k))

    def siblings(h, got, count, base):
        for j in range(count):
            width = 1 << j
            total = got[h, width]
            for k in range(width + 1, 2 * width):
                total = total + got[h, k]
            mean = (total * (1.0 / width)).astype(BF16)
            kc[h, pl.ds((base + j) * crows, crows), :] = mean[:crows]
            vc[h, pl.ds((base + j) * crows, crows), :] = mean[crows:]

    for h in range(2):
        drain(yr.at[h, pl.ds(1, ny - 1)], recv.at[S_YF + h])
        total = yr[h, 0]
        for k in range(1, ny):
            total = total + yr[h, k]
        zr[h, 0] = total * (1.0 / ny)
        for k in far_first(nz):
            remote(zr.at[h, 0], zr.at[h, k], S_ZF + h, z_dev(k))
        siblings(h, yr, ly, 0)
    row_level = lax.broadcasted_iota(jnp.int32, (levels * crows, 1), 0) // crows
    offsets = jnp.zeros((levels * crows, 1), F32)
    for j in range(levels):
        offsets = jnp.where(row_level == j, math.log(float(rows) * 2.0**j), offsets)

    nt = (((1,), (1,)), ((), ()))
    nn = (((1,), (0,)), ((), ()))
    tn = (((0,), (0,)), ((), ()))

    def dot(a, b, dims):
        return lax.dot_general(a, b, dims, preferred_element_type=F32)

    fine, coarse = pl.ds(0, shard), pl.ds(shard, levels * crows)

    def scores(h, between):
        hc = pl.ds(h * HD, HD)
        block = min(shard, 256)
        kf, vf = kr[:, hc], vr[:, hc]
        kcv, vcv = kc[h], vc[h]
        for b in range(shard // block):
            if b == shard // block - 1 and between is not None:
                between()
            br = pl.ds(b * block, block)
            q, g = qr[br, hc], gr[br, hc]
            sf = dot(kf, q, nt) * scale
            sc = dot(kcv, q, nt) * scale + offsets
            top = jnp.maximum(
                jnp.max(sf, axis=0, keepdims=True), jnp.max(sc, axis=0, keepdims=True)
            )
            pf, pc = jnp.exp(sf - top), jnp.exp(sc - top)
            norm = 1.0 / (
                jnp.sum(pf, axis=0, keepdims=True) + jnp.sum(pc, axis=0, keepdims=True)
            )
            pf, pc = pf * norm, pc * norm
            pk[fine, br] = pf.astype(BF16)
            pk[coarse, br] = pc.astype(BF16)
            df, dc = dot(vf, g, nt), dot(vcv, g, nt)
            delta = jnp.sum(pf * df, axis=0, keepdims=True) + jnp.sum(
                pc * dc, axis=0, keepdims=True
            )
            dsk[fine, br] = (scale * pf * (df - delta)).astype(BF16)
            dsk[coarse, br] = (scale * pc * (dc - delta)).astype(BF16)
        dkc[h] = dot(dsk[coarse, :], qr[:, hc], nn)
        dvc[h] = dot(pk[coarse, :], gr[:, hc], nn)

    def products(h):
        hc = pl.ds(h * HD, HD)
        kf, vf, kcv, vcv = kr[:, hc], vr[:, hc], kc[h], vc[h]
        os[h] = (dot(pk[fine, :], vf, tn) + dot(pk[coarse, :], vcv, tn)).astype(BF16)
        dqs[h] = (dot(dsk[fine, :], kf, tn) + dot(dsk[coarse, :], kcv, tn)).astype(BF16)
        dks[h] = dot(dsk[fine, :], qr[:, hc], nn).astype(BF16)
        dvs[h] = dot(pk[fine, :], gr[:, hc], nn).astype(BF16)

    def scatter_out(src, h, which):
        out = outs[which]
        start = pl.multiple_of((h_me * 2 + h) * HD, HD)
        there = out.at[:, pl.ds(start, HD)]
        for s in order:
            remote(src.at[h, pl.ds(s * rows, rows), :], there, S_OUT + which, (s_me, behind(s)))
        pltpu.make_async_copy(src.at[h, pl.ds(0, rows), :], there, recv.at[S_OUT + which]).start()

    def back_along_y(h):
        drain(zb.at[h, pl.ds(1, nz - 1)], recv.at[S_ZB + h])
        total = zb[h, 1].astype(F32)
        for k in range(2, nz):
            total = total + zb[h, k].astype(F32)
        za[h] = total
        for j in range(ly):
            at = pl.ds(j * crows, crows)
            weight = 2.0**-j
            key_part = total[:crows] + dkc[h, at, :] * weight
            value_part = total[crows:] + dvc[h, at, :] * weight
            ys[h, j, pl.ds(0, crows), :] = key_part.astype(BF16)
            ys[h, j, pl.ds(crows, crows), :] = value_part.astype(BF16)
        for k in far_first(ny):
            remote(ys.at[h, k.bit_length() - 1], yb.at[h, k], S_YB + h, y_dev(k))

    drain(kr, recv.at[S_K])
    drain(vr, recv.at[S_V])
    for h in range(2):
        drain(zr.at[h, pl.ds(1, nz - 1)], recv.at[S_ZF + h])
        siblings(h, zr, lz, ly)
        drain(qr.at[:, pl.ds(h * HD, HD)], recv.at[S_Q + h])
        drain(gr.at[:, pl.ds(h * HD, HD)], recv.at[S_G + h])
        scores(h, (lambda: back_along_y(0)) if h else None)
        for j in range(lz):
            at = pl.ds((ly + j) * crows, crows)
            weight = 2.0 ** -(ly + j)
            zs[h, j, pl.ds(0, crows), :] = (dkc[h, at, :] * weight).astype(BF16)
            zs[h, j, pl.ds(crows, crows), :] = (dvc[h, at, :] * weight).astype(BF16)
        for k in far_first(nz):
            remote(zs.at[h, k.bit_length() - 1], zb.at[h, k], S_ZB + h, z_dev(k))
        products(h)
        if h == 1:
            back_along_y(1)
        for which, staged in enumerate((os, dqs, dks, dvs)):
            if (h, which) != (1, 3):
                scatter_out(staged, h, which)

    for h in range(2):
        drain(yb.at[h, pl.ds(1, ny - 1)], recv.at[S_YB + h])
        total = za[h]
        for k in range(1, ny):
            total = total + yb[h, k].astype(F32)
        total = total * (1.0 / rows)
        gs[:, h * 2, :] = total[:crows]
        gs[:, h * 2 + 1, :] = total[crows:]
    for s in order:
        remote(gs.at[s], gx_out.at[h_me], S_GX, (s_me, behind(s)))
    pltpu.make_async_copy(gs.at[0], gx_out.at[h_me], recv.at[S_GX]).start()
    scatter_out(dvs, 1, 3)

    for which, out in enumerate(outs):
        drain(out, recv.at[S_OUT + which])
    drain(gx_out, recv.at[S_GX])

    drain(pr.at[pl.ds(1, nh - 1)], send.at[S_POOL])
    part = pl.ds(0, shard - rows)
    drain(kr.at[part], send.at[S_K])
    drain(vr.at[part], send.at[S_V])
    for h in range(2):
        hc = pl.ds(h * HD, HD)
        drain(qr.at[part, hc], send.at[S_Q + h])
        drain(gr.at[part, hc], send.at[S_G + h])
        drain(yr.at[h, pl.ds(1, ny - 1)], send.at[S_YF + h])
        drain(zr.at[h, pl.ds(1, nz - 1)], send.at[S_ZF + h])
        drain(zb.at[h, pl.ds(1, nz - 1)], send.at[S_ZB + h])
        drain(yb.at[h, pl.ds(1, ny - 1)], send.at[S_YB + h])
    for which in range(4):
        drain(kr.at[part], send.at[S_OUT + which])
    drain(gs.at[pl.ds(1, nh - 1)], send.at[S_GX])


def put_out(*refs):
    arrived, placed = refs[:5], refs[5:9]
    staged, pooled, sems = refs[9:]
    ins = [staged.at[i] for i in range(4)] + [pooled]
    first = [pltpu.make_async_copy(arrived[i], ins[i], sems.at[0, i]) for i in range(5)]
    last = [pltpu.make_async_copy(staged.at[i], placed[i], sems.at[1, i]) for i in range(4)]
    for copy in first:
        copy.start()
    for i in range(2):
        first[i].wait()
        last[i].start()
    first[4].wait()
    for kv in range(2):
        first[2 + kv].wait()
        for d in range(pooled.shape[0]):
            for h in range(2):
                cols = pl.ds((d * 2 + h) * HD, HD)
                row = pooled[d, pl.ds(h * 2 + kv, 1), :]
                staged[2 + kv, :, cols] = (staged[2 + kv, :, cols].astype(F32) + row).astype(BF16)
        last[2 + kv].start()
    for copy in last:
        copy.wait()


def solution(mesh):
    seq, head = mesh.shape["seq"], mesh.shape["head"]
    depth = seq.bit_length() - 1
    ny = 1 << (depth // 2)
    nz = seq // ny
    nx = head // 2

    def on_device(queries, keys_in, values_in, grad_out):
        rows, width = queries.shape
        shard = rows * head
        levels = depth
        here = jax.ShapeDtypeStruct((rows, width), BF16)
        anywhere = pl.BlockSpec(memory_space=pl.ANY)
        vm = pltpu.VMEM
        results = pl.pallas_call(
            functools.partial(kernel, (nx, ny, nz)),
            out_shape=(here,) * 4 + (jax.ShapeDtypeStruct((head, 4, HD), F32),),
            in_specs=[anywhere] * 4,
            out_specs=(anywhere,) * 5,
            scratch_shapes=[
                vm((rows, width), BF16),
                vm((rows, width), BF16),
                vm((head, 4, HD), F32),
                vm((head, 4, HD), F32),
                vm((shard, 2 * HD), BF16),
                vm((shard, 2 * HD), BF16),
                vm((shard, 2 * HD), BF16),
                vm((shard, 2 * HD), BF16),
                vm((2, ny, 2 * head, HD), F32),
                vm((2, nz, 2 * head, HD), F32),
                vm((2, levels * head, HD), BF16),
                vm((2, levels * head, HD), BF16),
                vm((2, depth - depth // 2, 2 * head, HD), BF16),
                vm((2, nz, 2 * head, HD), BF16),
                vm((2, depth // 2, 2 * head, HD), BF16),
                vm((2, ny, 2 * head, HD), BF16),
                vm((2, 2 * head, HD), F32),
                vm((shard + levels * head, shard), BF16),
                vm((shard + levels * head, shard), BF16),
                vm((head, 4, HD), F32),
                vm((2, shard, HD), BF16),
                vm((2, shard, HD), BF16),
                vm((2, shard, HD), BF16),
                vm((2, shard, HD), BF16),
                vm((2, levels * head, HD), F32),
                vm((2, levels * head, HD), F32),
                pltpu.SemaphoreType.DMA((2,)),
                pltpu.SemaphoreType.DMA((N_SEMS,)),
                pltpu.SemaphoreType.DMA((N_SEMS,)),
                pltpu.SemaphoreType.REGULAR,
            ],
            compiler_params=pltpu.CompilerParams(
                collective_id=0, has_side_effects=True, vmem_limit_bytes=67043328
            ),
        )(queries, keys_in, values_in, grad_out)
        return pl.pallas_call(
            put_out,
            out_shape=(here,) * 4,
            in_specs=[anywhere] * 5,
            out_specs=(anywhere,) * 4,
            scratch_shapes=[
                vm((4, rows, width), BF16),
                vm((head, 4, HD), F32),
                pltpu.SemaphoreType.DMA((2, 5)),
            ],
            compiler_params=pltpu.CompilerParams(vmem_limit_bytes=67043328),
        )(*results)

    placed = P(("seq", "head"), None)
    return jax.shard_map(
        on_device, mesh=mesh, in_specs=(placed,) * 4, out_specs=(placed,) * 4, check_vma=False
    )
```

```python
import functools
import math

import jax
import jax.numpy as jnp
from jax import lax
from jax.experimental import pallas as pl
from jax.experimental.pallas import tpu as pltpu
from jax.sharding import PartitionSpec as P

HD = 128
MESH = pl.DeviceIdType.MESH
F32 = jnp.float32
BF16 = jnp.bfloat16

S_POOL, S_K, S_V, S_Q, S_G, S_YF, S_ZF, S_ZB, S_YB, S_OUT, S_GX = 0, 1, 2, 3, 5, 7, 9, 11, 13, 15, 19
N_SEMS = 20


def flip(index, mask):
    out = index
    bit = 1
    while bit <= mask:
        if mask & bit:
            out = out + bit * (1 - 2 * ((index // bit) % 2))
        bit *= 2
    return out


def kernel(sizes, *refs):
    nx, ny, nz = sizes
    (q_in, k_in, v_in, g_in, o_out, dq_out, dk_out, dv_out, gx_out,
     kl, vl, ps, pr, qr, kr, vr, gr, yr, zr, kc, vc, zs, zb, ys, yb,
     za, pk, dsk, gs, os, dqs, dks, dvs, dkc, dvc, local_sem, send, recv, go) = refs
    ins = (q_in, k_in, v_in, g_in)
    outs = (o_out, dq_out, dk_out, dv_out)
    nh = nx * 2
    rows = q_in.shape[0]
    shard = nh * rows
    ly, lz = ny.bit_length() - 1, nz.bit_length() - 1
    levels = ly + lz
    crows = nh
    scale = HD ** (-0.5)

    s_me = lax.axis_index("seq")
    h_me = lax.axis_index("head")
    y_me, z_me = s_me % ny, s_me // ny
    x_me, c_me = h_me // 2, h_me % 2

    def ahead(slot):
        k, f = slot // 2, slot % 2
        return ((x_me + k) % nx) * 2 + (c_me if f == 0 else 1 - c_me)

    def behind(slot):
        k, f = slot // 2, slot % 2
        return ((x_me + nx - k) % nx) * 2 + (c_me if f == 0 else 1 - c_me)

    order = []
    for k in range(nx // 2, -1, -1):
        for kk in dict.fromkeys((k, (nx - k) % nx)):
            order += [2 * kk, 2 * kk + 1]
    order = [s for s in order if s != 0]

    def far_first(count):
        return sorted(range(1, count), key=lambda k: (-min(k, count - k), k))

    def y_dev(k):
        return (z_me * ny + flip(y_me, k), h_me)

    def z_dev(k):
        return (flip(z_me, k) * ny + y_me, h_me)

    kcopy = pltpu.make_async_copy(k_in, kl, local_sem.at[0])
    vcopy = pltpu.make_async_copy(v_in, vl, local_sem.at[1])
    kcopy.start()
    vcopy.start()

    barrier = pltpu.get_barrier_semaphore()
    for s in order:
        pl.semaphore_signal(barrier, inc=1, device_id=(s_me, ahead(s)), device_id_type=MESH)

    kcopy.wait()
    vcopy.wait()
    for d in range(nh):
        for h in range(2):
            cols = pl.ds((d * 2 + h) * HD, HD)
            for kv, ref in enumerate((kl, vl)):
                mean = jnp.sum(ref[:, cols].astype(F32), axis=0, keepdims=True) * (1.0 / rows)
                ps[d, pl.ds(h * 2 + kv, 1), :] = mean

    lines = [y_dev(k)[0] for k in range(1, ny)] + [z_dev(k)[0] for k in range(1, nz)]
    pl.semaphore_wait(barrier, len(order) + jnp.where(h_me == 0, len(lines), 0))

    @pl.when(h_me == 1)
    def _():
        for line in lines:
            pl.semaphore_signal(barrier, inc=1, device_id=(line, 0), device_id_type=MESH)

    @pl.when(h_me == 0)
    def _():
        for d in range(1, nh):
            pl.semaphore_signal(go, inc=1, device_id=(s_me, d), device_id_type=MESH)

    def remote(src, dst, sem, device):
        pltpu.make_async_remote_copy(
            src_ref=src, dst_ref=dst, send_sem=send.at[sem], recv_sem=recv.at[sem],
            device_id=device, device_id_type=MESH,
        ).start()

    def drain(ref, sem):
        pltpu.make_async_copy(ref, ref, sem).wait()

    def scatter_in(src, dst, sem, first, width):
        def piece(d):
            start = pl.multiple_of(d * 2 * HD + first, HD)
            return src.at[:, pl.ds(start, width)]

        for s in order:
            d = ahead(s)
            remote(piece(d), dst.at[pl.ds(s * rows, rows), pl.ds(first, width)], sem, (s_me, d))
        pltpu.make_async_copy(
            piece(h_me), dst.at[pl.ds(0, rows), pl.ds(first, width)], recv.at[sem]
        ).start()

    for s in order:
        d = ahead(s)
        remote(ps.at[d], pr.at[s], S_POOL, (s_me, d))
    pr[0] = ps[h_me]

    scatter_in(k_in, kr, S_K, 0, 2 * HD)
    scatter_in(v_in, vr, S_V, 0, 2 * HD)
    for h in range(2):
        scatter_in(q_in, qr, S_Q + h, h * HD, HD)
        scatter_in(g_in, gr, S_G + h, h * HD, HD)

    drain(pr.at[pl.ds(1, nh - 1)], recv.at[S_POOL])

    @pl.when(h_me != 0)
    def _():
        pl.semaphore_wait(go, 1)

    for h in range(2):
        for kv in range(2):
            yr[h, 0, pl.ds(kv * crows, crows), :] = pr[:, h * 2 + kv, :]
        for k in far_first(ny):
            remote(yr.at[h, 0], yr.at[h, k], S_YF + h, y_dev(k))

    def siblings(h, got, count, base):
        for j in range(count):
            width = 1 << j
            total = got[h, width]
            for k in range(width + 1, 2 * width):
                total = total + got[h, k]
            mean = (total * (1.0 / width)).astype(BF16)
            kc[h, pl.ds((base + j) * crows, crows), :] = mean[:crows]
            vc[h, pl.ds((base + j) * crows, crows), :] = mean[crows:]

    for h in range(2):
        drain(yr.at[h, pl.ds(1, ny - 1)], recv.at[S_YF + h])
        total = yr[h, 0]
        for k in range(1, ny):
            total = total + yr[h, k]
        zr[h, 0] = total * (1.0 / ny)
        for k in far_first(nz):
            remote(zr.at[h, 0], zr.at[h, k], S_ZF + h, z_dev(k))
        siblings(h, yr, ly, 0)
    row_level = lax.broadcasted_iota(jnp.int32, (levels * crows, 1), 0) // crows
    offsets = jnp.zeros((levels * crows, 1), F32)
    for j in range(levels):
        offsets = jnp.where(row_level == j, math.log(float(rows) * 2.0**j), offsets)

    nt = (((1,), (1,)), ((), ()))
    nn = (((1,), (0,)), ((), ()))
    tn = (((0,), (0,)), ((), ()))

    def dot(a, b, dims):
        return lax.dot_general(a, b, dims, preferred_element_type=F32)

    fine, coarse = pl.ds(0, shard), pl.ds(shard, levels * crows)

    def scores(h, between):
        hc = pl.ds(h * HD, HD)
        block = min(shard, 256)
        kf, vf = kr[:, hc], vr[:, hc]
        kcv, vcv = kc[h], vc[h]
        for b in range(shard // block):
            if b == shard // block - 1 and between is not None:
                between()
            br = pl.ds(b * block, block)
            q, g = qr[br, hc], gr[br, hc]
            sf = dot(kf, q, nt) * scale
            sc = dot(kcv, q, nt) * scale + offsets
            top = jnp.maximum(
                jnp.max(sf, axis=0, keepdims=True), jnp.max(sc, axis=0, keepdims=True)
            )
            pf, pc = jnp.exp(sf - top), jnp.exp(sc - top)
            norm = 1.0 / (
                jnp.sum(pf, axis=0, keepdims=True) + jnp.sum(pc, axis=0, keepdims=True)
            )
            pf, pc = pf * norm, pc * norm
            pk[fine, br] = pf.astype(BF16)
            pk[coarse, br] = pc.astype(BF16)
            df, dc = dot(vf, g, nt), dot(vcv, g, nt)
            delta = jnp.sum(pf * df, axis=0, keepdims=True) + jnp.sum(
                pc * dc, axis=0, keepdims=True
            )
            dsk[fine, br] = (scale * pf * (df - delta)).astype(BF16)
            dsk[coarse, br] = (scale * pc * (dc - delta)).astype(BF16)
        dkc[h] = dot(dsk[coarse, :], qr[:, hc], nn)
        dvc[h] = dot(pk[coarse, :], gr[:, hc], nn)

    def products(h):
        hc = pl.ds(h * HD, HD)
        kf, vf, kcv, vcv = kr[:, hc], vr[:, hc], kc[h], vc[h]
        os[h] = (dot(pk[fine, :], vf, tn) + dot(pk[coarse, :], vcv, tn)).astype(BF16)
        dqs[h] = (dot(dsk[fine, :], kf, tn) + dot(dsk[coarse, :], kcv, tn)).astype(BF16)
        dks[h] = dot(dsk[fine, :], qr[:, hc], nn).astype(BF16)
        dvs[h] = dot(pk[fine, :], gr[:, hc], nn).astype(BF16)

    def scatter_out(src, h, which):
        out = outs[which]
        start = pl.multiple_of((h_me * 2 + h) * HD, HD)
        there = out.at[:, pl.ds(start, HD)]
        for s in order:
            remote(src.at[h, pl.ds(s * rows, rows), :], there, S_OUT + which, (s_me, behind(s)))
        pltpu.make_async_copy(src.at[h, pl.ds(0, rows), :], there, recv.at[S_OUT + which]).start()

    def back_along_y(h):
        drain(zb.at[h, pl.ds(1, nz - 1)], recv.at[S_ZB + h])
        total = zb[h, 1].astype(F32)
        for k in range(2, nz):
            total = total + zb[h, k].astype(F32)
        za[h] = total
        for j in range(ly):
            at = pl.ds(j * crows, crows)
            weight = 2.0**-j
            key_part = total[:crows] + dkc[h, at, :] * weight
            value_part = total[crows:] + dvc[h, at, :] * weight
            ys[h, j, pl.ds(0, crows), :] = key_part.astype(BF16)
            ys[h, j, pl.ds(crows, crows), :] = value_part.astype(BF16)
        for k in far_first(ny):
            remote(ys.at[h, k.bit_length() - 1], yb.at[h, k], S_YB + h, y_dev(k))

    drain(kr, recv.at[S_K])
    drain(vr, recv.at[S_V])
    for h in range(2):
        drain(zr.at[h, pl.ds(1, nz - 1)], recv.at[S_ZF + h])
        siblings(h, zr, lz, ly)
        drain(qr.at[:, pl.ds(h * HD, HD)], recv.at[S_Q + h])
        drain(gr.at[:, pl.ds(h * HD, HD)], recv.at[S_G + h])
        scores(h, None)
        for j in range(lz):
            at = pl.ds((ly + j) * crows, crows)
            weight = 2.0 ** -(ly + j)
            zs[h, j, pl.ds(0, crows), :] = (dkc[h, at, :] * weight).astype(BF16)
            zs[h, j, pl.ds(crows, crows), :] = (dvc[h, at, :] * weight).astype(BF16)
        for k in far_first(nz):
            remote(zs.at[h, k.bit_length() - 1], zb.at[h, k], S_ZB + h, z_dev(k))
        if h == 1:
            back_along_y(0)
        products(h)
        if h == 1:
            back_along_y(1)
        for which, staged in enumerate((os, dqs, dks, dvs)):
            if (h, which) != (1, 3):
                scatter_out(staged, h, which)

    for h in range(2):
        drain(yb.at[h, pl.ds(1, ny - 1)], recv.at[S_YB + h])
        total = za[h]
        for k in range(1, ny):
            total = total + yb[h, k].astype(F32)
        total = total * (1.0 / rows)
        gs[:, h * 2, :] = total[:crows]
        gs[:, h * 2 + 1, :] = total[crows:]
    for s in order:
        remote(gs.at[s], gx_out.at[h_me], S_GX, (s_me, behind(s)))
    pltpu.make_async_copy(gs.at[0], gx_out.at[h_me], recv.at[S_GX]).start()
    scatter_out(dvs, 1, 3)

    for which, out in enumerate(outs):
        drain(out, recv.at[S_OUT + which])
    drain(gx_out, recv.at[S_GX])

    drain(pr.at[pl.ds(1, nh - 1)], send.at[S_POOL])
    part = pl.ds(0, shard - rows)
    drain(kr.at[part], send.at[S_K])
    drain(vr.at[part], send.at[S_V])
    for h in range(2):
        hc = pl.ds(h * HD, HD)
        drain(qr.at[part, hc], send.at[S_Q + h])
        drain(gr.at[part, hc], send.at[S_G + h])
        drain(yr.at[h, pl.ds(1, ny - 1)], send.at[S_YF + h])
        drain(zr.at[h, pl.ds(1, nz - 1)], send.at[S_ZF + h])
        drain(zb.at[h, pl.ds(1, nz - 1)], send.at[S_ZB + h])
        drain(yb.at[h, pl.ds(1, ny - 1)], send.at[S_YB + h])
    for which in range(4):
        drain(kr.at[part], send.at[S_OUT + which])
    drain(gs.at[pl.ds(1, nh - 1)], send.at[S_GX])


def put_out(*refs):
    arrived, placed = refs[:5], refs[5:9]
    staged, pooled, sems = refs[9:]
    ins = [staged.at[i] for i in range(4)] + [pooled]
    first = [pltpu.make_async_copy(arrived[i], ins[i], sems.at[0, i]) for i in range(5)]
    last = [pltpu.make_async_copy(staged.at[i], placed[i], sems.at[1, i]) for i in range(4)]
    for copy in first:
        copy.start()
    for i in range(2):
        first[i].wait()
        last[i].start()
    first[4].wait()
    for kv in range(2):
        first[2 + kv].wait()
        for d in range(pooled.shape[0]):
            for h in range(2):
                cols = pl.ds((d * 2 + h) * HD, HD)
                row = pooled[d, pl.ds(h * 2 + kv, 1), :]
                staged[2 + kv, :, cols] = (staged[2 + kv, :, cols].astype(F32) + row).astype(BF16)
        last[2 + kv].start()
    for copy in last:
        copy.wait()


def solution(mesh):
    seq, head = mesh.shape["seq"], mesh.shape["head"]
    depth = seq.bit_length() - 1
    ny = 1 << (depth // 2)
    nz = seq // ny
    nx = head // 2

    def on_device(queries, keys_in, values_in, grad_out):
        rows, width = queries.shape
        shard = rows * head
        levels = depth
        here = jax.ShapeDtypeStruct((rows, width), BF16)
        anywhere = pl.BlockSpec(memory_space=pl.ANY)
        vm = pltpu.VMEM
        results = pl.pallas_call(
            functools.partial(kernel, (nx, ny, nz)),
            out_shape=(here,) * 4 + (jax.ShapeDtypeStruct((head, 4, HD), F32),),
            in_specs=[anywhere] * 4,
            out_specs=(anywhere,) * 5,
            scratch_shapes=[
                vm((rows, width), BF16),
                vm((rows, width), BF16),
                vm((head, 4, HD), F32),
                vm((head, 4, HD), F32),
                vm((shard, 2 * HD), BF16),
                vm((shard, 2 * HD), BF16),
                vm((shard, 2 * HD), BF16),
                vm((shard, 2 * HD), BF16),
                vm((2, ny, 2 * head, HD), F32),
                vm((2, nz, 2 * head, HD), F32),
                vm((2, levels * head, HD), BF16),
                vm((2, levels * head, HD), BF16),
                vm((2, depth - depth // 2, 2 * head, HD), BF16),
                vm((2, nz, 2 * head, HD), BF16),
                vm((2, depth // 2, 2 * head, HD), BF16),
                vm((2, ny, 2 * head, HD), BF16),
                vm((2, 2 * head, HD), F32),
                vm((shard + levels * head, shard), BF16),
                vm((shard + levels * head, shard), BF16),
                vm((head, 4, HD), F32),
                vm((2, shard, HD), BF16),
                vm((2, shard, HD), BF16),
                vm((2, shard, HD), BF16),
                vm((2, shard, HD), BF16),
                vm((2, levels * head, HD), F32),
                vm((2, levels * head, HD), F32),
                pltpu.SemaphoreType.DMA((2,)),
                pltpu.SemaphoreType.DMA((N_SEMS,)),
                pltpu.SemaphoreType.DMA((N_SEMS,)),
                pltpu.SemaphoreType.REGULAR,
            ],
            compiler_params=pltpu.CompilerParams(
                collective_id=0, has_side_effects=True, vmem_limit_bytes=67043328
            ),
        )(queries, keys_in, values_in, grad_out)
        return pl.pallas_call(
            put_out,
            out_shape=(here,) * 4,
            in_specs=[anywhere] * 5,
            out_specs=(anywhere,) * 4,
            scratch_shapes=[
                vm((4, rows, width), BF16),
                vm((head, 4, HD), F32),
                pltpu.SemaphoreType.DMA((2, 5)),
            ],
            compiler_params=pltpu.CompilerParams(vmem_limit_bytes=67043328),
        )(*results)

    placed = P(("seq", "head"), None)
    return jax.shard_map(
        on_device, mesh=mesh, in_specs=(placed,) * 4, out_specs=(placed,) * 4, check_vma=False
    )
```
